128 devices in a mesh: omega: 16 (over x, y_hi, core), row: 4 (over z), col: 2 (over y_lo).
Axes of the slice: x: 4, y: 4 (y_hi: 2, y_lo: 2; y = y_hi * 2 + y_lo), z: 4, core: 2. Of those that a mesh axis runs over, the one named last changes fastest.
Arguments:
- frames: bfloat16 [2, 256, 512, 2048], P(None, 'omega', 'row', 'col'), may hold values from -6 to 6
- omega_taps: float32 [15], replicated, may hold values from 0.1 to 1
- smooth_kernel: float32 [5, 5], replicated, may hold values from 0.05 to 0.15
- spots: int32 [2, 3, 16384], P(None, None, ('omega', 'row', 'col')), may hold values from 0 to 2032, as said below
- counts: int32 [2, 128], P(None, ('omega', 'row', 'col')), may hold values from 1 to 128, as said below
Outputs:
- smoothed: bfloat16 [2, 256, 512, 2048], P(None, 'omega', 'row', 'col')
- scores: float32 [16384, 128], P(('omega', 'row', 'col'))
The draws below stay inside these ranges and needn't reach their ends.
Inputs may be any that keep to these rules, and one draw needn't show every extreme that they name: `spots`: slot i belongs to block i div 128; its spot's frame lies in that block's frames and its whole 16 x 16 patch lies in that block's rows and columns. `counts`: some block of each slab has all 128 slots live.
All inputs are finite; a program needn't handle non-finite values.
Results may differ from the reference program's by a relative error of at most 0.0022.
Values may be sent and summed in bfloat16 or wider, within the bound.
A program may use at most 192 MiB of HBM per device.

```python
import math
import jax
import jax.numpy as jnp
from jax import lax

FD = 16
RD = 128
CD = 1024
K = 128
TAPS = 15
PATCH = 16
FRAMES = 256
ROWS = 512
COLS = 2048
BANDS = 4
HALVES = 2
BLOCKS = 128
N_OMEGA = 16
N_ROW = 4
N_COL = 2


def draw_spots(key, part):
    slot_total = K * BLOCKS
    block = jnp.arange(slot_total, dtype=jnp.int32) // K
    frame_block = block // (BANDS * HALVES)
    band = block // HALVES % BANDS
    half = block % HALVES
    key_frame, key_row, key_col = jax.random.split(key, 3)
    frame_off = jax.random.randint(key_frame, (2, slot_total), 0, FD)
    row_off = jax.random.randint(key_row, (2, slot_total), 0, RD - PATCH + 1)
    col_off = jax.random.randint(key_col, (2, slot_total), 0, CD - PATCH + 1)
    frame_off = frame_off.at[:, 0].set(0).at[:, slot_total - 1].set(FD - 1)
    row_off = row_off.at[:, 0].set(0).at[:, slot_total - 1].set(RD - PATCH)
    col_off = col_off.at[:, 0].set(0).at[:, slot_total - 1].set(CD - PATCH)
    frame = frame_block * FD + frame_off
    row = band * RD + row_off
    col = half * CD + col_off
    return jnp.stack([frame, row, col], axis=1).astype(jnp.int32)


def draw_counts(key, part):
    key_base, key_top = jax.random.split(key)
    base = jax.random.randint(key_base, (2, BLOCKS), max(1, K // 8), K + 1)
    top = jax.random.randint(key_top, (2,), 0, BLOCKS)
    return base.at[jnp.arange(2), top].set(K).astype(jnp.int32)


def steps_of(stream_key, extent, cuts, low, largest):
    def one(axis_at, shards_of):
        draws = jax.random.uniform(jax.random.fold_in(jax.random.fold_in(stream_key, 6), axis_at), (shards_of,), jnp.float32, low / len(cuts), largest / len(cuts))
        return jnp.repeat(jnp.exp(draws), extent[axis_at] // shards_of).reshape((-1,) + (1,) * (len(extent) - axis_at - 1))

    factor_of = one(*cuts[0])
    for cut in cuts[1:]:
        factor_of = factor_of * one(*cut)
    return factor_of


def gaussian(key, shape, width, bound, pieces=(), kind=jnp.bfloat16):
    values = jax.random.normal(key, shape, jnp.float32) * width
    if len(pieces) > 0:
        values = steps_of(key, shape, pieces, -0.22, 0.18) * values
    return jnp.clip(values, min=-bound, max=bound).astype(kind)


def setup_inputs(seed: int = 0) -> dict:
    arg_keys = jax.random.split(jax.random.key(seed), 6)
    frames = gaussian(arg_keys[0], (2, FRAMES, ROWS, COLS), 1.0, 6.0, ((1, 16), (2, 4), (3, 2)))
    omega_taps = jnp.clip(jnp.exp(jax.random.uniform(arg_keys[1], (TAPS,), jnp.float32, math.log(0.1), math.log(1.0))), 0.1, 1.0)
    smooth_kernel = jnp.clip(jax.random.uniform(arg_keys[2], (5, 5), jnp.float32, 0.05, 0.15), 0.05, 0.15)
    spots = draw_spots(jax.random.fold_in(arg_keys[5], 71), 0)
    counts = draw_counts(jax.random.fold_in(arg_keys[5], 71), 0)
    return dict(frames=frames, omega_taps=omega_taps, smooth_kernel=smooth_kernel, spots=spots, counts=counts)


def normalize(values, live):
    mean_value = lax.optimization_barrier(jnp.mean(values, axis=1, keepdims=True))
    centered = values - mean_value
    spread = lax.optimization_barrier(jnp.mean(centered * centered, axis=1, keepdims=True))
    normed = centered / jnp.sqrt(spread + 1e-05)
    return jnp.where(live[:, None], normed, 0.0).astype(jnp.bfloat16)

def reference(frames, omega_taps, smooth_kernel, spots, counts):
    frame_total = frames.shape[1]
    row_total = frames.shape[2]
    col_total = frames.shape[3]

    def one_frame(index):
        slab = (index // frame_total).astype(jnp.int32)
        frame = (index % frame_total).astype(jnp.int32)
        center = lax.dynamic_slice(frames, (slab, frame, jnp.int32(0), jnp.int32(0)), (1, 1, row_total, col_total))[0, 0].astype(jnp.float32)
        background = jnp.zeros((row_total, col_total), jnp.float32)
        norm = jnp.float32(0.0)
        for offset in range(TAPS):
            source = frame + offset - 7
            valid = ((source >= 0) & (source < frame_total)).astype(jnp.float32)
            clipped = jnp.clip(source, 0, frame_total - 1).astype(jnp.int32)
            plane = lax.dynamic_slice(frames, (slab, clipped, jnp.int32(0), jnp.int32(0)), (1, 1, row_total, col_total))[0, 0].astype(jnp.float32)
            background = background + omega_taps[offset] * valid * plane
            norm = norm + omega_taps[offset] * valid
        corrected = center - background / norm
        padded = jnp.pad(corrected, 2)
        result = jnp.zeros((row_total, col_total), jnp.float32)
        for row_shift in range(5):
            for col_shift in range(5):
                result = result + smooth_kernel[row_shift, col_shift] * padded[row_shift:row_shift + row_total, col_shift:col_shift + col_total]
        return result.astype(jnp.bfloat16)
    flat = lax.map(one_frame, jnp.arange(2 * frame_total, dtype=jnp.int32))
    smoothed = flat.reshape(2, frame_total, row_total, col_total)
    slot_total = spots.shape[2]
    slot_ids = jnp.arange(slot_total, dtype=jnp.int32)

    def patches_of(slab):

        def take(frame, row, col):
            return lax.dynamic_slice(smoothed[slab], (frame, row, col), (1, PATCH, PATCH)).reshape(PATCH * PATCH)
        values = jax.vmap(take)(spots[slab, 0], spots[slab, 1], spots[slab, 2]).astype(jnp.float32)
        live = slot_ids % K < counts[slab][slot_ids // K]
        return normalize(values, live)
    first = patches_of(0).reshape(N_OMEGA, N_ROW * N_COL, K, PATCH * PATCH)
    second = patches_of(1).reshape(N_OMEGA, N_ROW * N_COL, K, PATCH * PATCH)[:, ::-1]
    scores = jnp.einsum('obik,objk->obij', first.astype(jnp.float32), second.astype(jnp.float32)) / 256.0
    return (smoothed, scores.reshape(slot_total, K))
```

```python
import functools

import jax
import jax.numpy as jnp
from jax import lax
from jax.experimental import pallas as pl
from jax.experimental.pallas import tpu as pltpu
from jax.sharding import PartitionSpec as P

TAPS = 15
PATCH = 16
HALF = 7
LANES = 128
MESH = pl.DeviceIdType.MESH
F32 = jnp.float32
BF16 = jnp.bfloat16


def normalize_patches(held, spots, counts, slab, windows, patches, normed, by_amount):
    n_frame, n_r, n_c = held.shape
    n_slot = normed.shape[0]
    lane = lax.broadcasted_iota(jnp.int32, (24, LANES), 1)
    group = lax.broadcasted_iota(jnp.int32, (n_slot, LANES), 1)
    slot = lax.broadcasted_iota(jnp.int32, (n_slot, 1), 0)

    def one(i, _):
        f = spots[0, slab, i] & (n_frame - 1)
        row = spots[1, slab, i] & (n_r - 1)
        col = spots[2, slab, i] & (n_c - 1)
        row_0 = jnp.minimum(row >> 3, n_r // 8 - 3) * 8
        col_0 = jnp.minimum(col >> 7, n_c // LANES - 2) * LANES
        shift = col - col_0
        window = held[f, pl.ds(row_0, 24), pl.ds(col_0, 2 * LANES)].astype(F32)
        left, right = window[:, :LANES], window[:, LANES:]
        if by_amount:
            turn = (2 * LANES - shift) & (LANES - 1)
            left = jnp.where(
                lane < LANES - shift, pltpu.roll(left, turn, 1), pltpu.roll(right, turn, 1)
            )
        else:
            left = jnp.where(shift >= LANES, right, left)
            for bit in (64, 32, 16, 8, 4, 2, 1):
                on = (shift & bit) != 0
                moved_left = pltpu.roll(left, LANES - bit, 1)
                moved_right = pltpu.roll(right, LANES - bit, 1)
                left = jnp.where(on, jnp.where(lane < LANES - bit, moved_left, moved_right), left)
                right = jnp.where(on, moved_right, right)
        at_window = (i & 7) * 24
        windows[pl.ds(at_window, 24)] = left
        patches[pl.ds(i * PATCH, PATCH)] = windows[pl.ds(at_window + (row - row_0), PATCH)]
        return 0

    lax.fori_loop(0, n_slot, one, 0, unroll=8)
    halves = []
    for half in range(2):
        total = jnp.zeros((n_slot, LANES), F32)
        for u in range(8):
            line = patches[pl.ds(half * 8 + u, n_slot, stride=PATCH)]
            line = pltpu.roll(line, PATCH * u, 1) if u else line
            total = jnp.where(
                jnp.logical_and(group >= PATCH * u, group < PATCH * (u + 1)), line, total
            )
        halves.append(total)
    values = jnp.concatenate(halves, axis=1)
    mean = jnp.mean(values, axis=1, keepdims=True)
    centered = values - mean
    spread = jnp.mean(centered * centered, axis=1, keepdims=True)
    result = centered / jnp.sqrt(spread + 1e-05)
    normed[...] = jnp.where(slot < counts[0, slab], result, 0.0).astype(BF16)


def layer_kernel(
    sizes,
    frames,
    taps,
    weights,
    spots,
    counts,
    own_0,
    own_1,
    mirror,
    ext_0,
    ext_1,
    slow_out,
    slow_in,
    rows_in,
    edge,
    strip,
    strip_in,
    side,
    bands,
    shifted_0,
    shifted_1,
    inverse,
    load_sem,
    edge_sem,
    rows_send,
    rows_recv,
    strip_send,
    strip_recv,
    slow_send,
    slow_recv,
    fast_send,
    fast_recv,
    windows,
    patches,
    normed,
    mirror_send,
    mirror_recv,
):
    n_omega, n_row, n_frame, n_r, n_c = sizes
    shifted = (shifted_0, shifted_1)
    ext = (ext_0, ext_1)
    own = (own_0, own_1)
    tiles = n_c // LANES
    o = lax.axis_index("omega")
    r = lax.axis_index("row")
    c = lax.axis_index("col")
    odd = lax.rem(o, 2)
    slow_o = o - 1 + 2 * odd
    fast_o = o + 1 - 2 * odd
    has_slow = jnp.logical_and(slow_o >= 0, slow_o < n_omega)
    has_up = r > 0
    has_down = r < n_row - 1

    def at(omega=o, row=r, col=c):
        return {"omega": omega, "row": row, "col": col}

    def slow_frame(j):
        return j + odd * (n_frame - 1 - 2 * j)

    def fast_frame(j):
        return slow_frame(n_frame - 1 - j)

    cuts = (0, 2, HALF, n_frame)
    order = [(slab, part) for slab in (1, 0) for part in range(3)]

    def stretch(part):
        start, stop = cuts[part], cuts[part + 1]
        return start + odd * (n_frame - stop - start), stop - start

    def edge_copy(slab):
        return pltpu.make_async_copy(
            frames.at[slab, :, :, pl.ds(pl.multiple_of((1 - c) * (n_c - LANES), LANES), LANES)],
            edge.at[slab],
            edge_sem.at[slab],
        )

    for slab in (1, 0):
        edge_copy(slab).start()

    def load(part, slab):
        first, count = stretch(part)
        return pltpu.make_async_copy(
            frames.at[slab, pl.ds(first, count)],
            own[slab].at[pl.ds(first, count)],
            load_sem.at[part, slab],
        )

    barrier = pltpu.get_barrier_semaphore()

    def greet(device):
        pl.semaphore_signal(barrier, inc=1, device_id=device, device_id_type=MESH)

    greet(at(omega=fast_o))
    greet(at(col=1 - c))
    greet(at(row=n_row - 1 - r, col=1 - c))

    @pl.when(has_slow)
    def _():
        greet(at(omega=slow_o))

    @pl.when(has_up)
    def _():
        greet(at(row=r - 1))
        greet(at(row=r - 1, col=1 - c))

    @pl.when(has_down)
    def _():
        greet(at(row=r + 1))
        greet(at(row=r + 1, col=1 - c))

    lane = lax.broadcasted_iota(jnp.int32, (n_r, LANES), 1)

    def pack(slab):
        edge_copy(slab).wait()

        def gather(f, packed):
            moved = pltpu.roll(edge[slab, f].astype(F32), 2 * f + 2 * (1 - c), 1)
            return jnp.where(jnp.logical_and(lane >= 2 * f, lane < 2 * f + 2), moved, packed)

        packed = lax.fori_loop(0, n_frame, gather, jnp.zeros((n_r, LANES), F32), unroll=4)
        strip[slab] = packed.astype(BF16)

    pack(1)
    pl.semaphore_wait(
        barrier,
        3
        + has_slow.astype(jnp.int32)
        + 2 * has_up.astype(jnp.int32)
        + 2 * has_down.astype(jnp.int32),
    )

    def strip_copy(which, slab):
        source, target, row = (
            (pl.ds(0, n_r), pl.ds(0, n_r), r),
            (pl.ds(0, 8), pl.ds(n_r + 8, 8), r - 1),
            (pl.ds(n_r - 8, 8), pl.ds(n_r, 8), r + 1),
        )[which]
        return pltpu.make_async_remote_copy(
            src_ref=strip.at[slab, source],
            dst_ref=strip_in.at[slab, target],
            send_sem=strip_send.at[which, slab],
            recv_sem=strip_recv.at[which, slab],
            device_id=at(row=row, col=1 - c),
            device_id_type=MESH,
        )

    def each_strip(slab, act):
        act(strip_copy(0, slab))

        @pl.when(has_up)
        def _():
            act(strip_copy(1, slab))

        @pl.when(has_down)
        def _():
            act(strip_copy(2, slab))

    def wait_strips(slab):
        strip_copy(0, slab).wait_recv()

        @pl.when(has_down)
        def _():
            strip_copy(1, slab).wait_recv()

        @pl.when(has_up)
        def _():
            strip_copy(2, slab).wait_recv()

    each_strip(1, lambda copy: copy.start())

    def rows_copy(part, slab, down):
        first, count = stretch(part)
        return pltpu.make_async_remote_copy(
            src_ref=frames.at[slab, pl.ds(first, count), pl.ds((n_r - 8) * down, 8)],
            dst_ref=rows_in.at[slab, pl.ds(first, count), pl.ds(8 * (1 - down), 8)],
            send_sem=rows_send.at[down, part, slab],
            recv_sem=rows_recv.at[1 - down, part, slab],
            device_id=at(row=r + 2 * down - 1),
            device_id_type=MESH,
        )

    for slab, part in order:

        @pl.when(has_up)
        def _():
            rows_copy(part, slab, 0).start()

        @pl.when(has_down)
        def _():
            rows_copy(part, slab, 1).start()

    for slab, part in order:
        load(part, slab).start()
    pack(0)
    each_strip(0, lambda copy: copy.start())

    @pl.when(jnp.logical_not(has_up))
    def _():
        rows_in[:, :, pl.ds(0, 8)] = jnp.zeros((2, n_frame, 8, n_c), BF16)
        strip_in[:, pl.ds(n_r, 8)] = jnp.zeros((2, 8, LANES), BF16)

    @pl.when(jnp.logical_not(has_down))
    def _():
        rows_in[:, :, pl.ds(8, 8)] = jnp.zeros((2, n_frame, 8, n_c), BF16)
        strip_in[:, pl.ds(n_r + 8, 8)] = jnp.zeros((2, 8, LANES), BF16)

    for f in range(n_frame):
        norm = jnp.zeros((8, LANES), F32)
        for t in range(TAPS):
            source = o * n_frame + (f + t - HALF)
            valid = jnp.logical_and(source >= 0, source < n_omega * n_frame)
            norm = norm + jnp.where(valid, taps[t], 0.0)
        inverse[f] = 1.0 / norm

    half = n_r // 2
    depth = half + 32
    to = lax.broadcasted_iota(jnp.int32, (half, depth), 0)
    source = lax.broadcasted_iota(jnp.int32, (half, depth), 1)
    top = jnp.where(source < half + 16, source, source - (half + 24))
    bottom = jnp.where(source < half + 16, source - 16, source - 24)
    upper = jnp.where(source < half + 24, top, n_r * 2) - to
    lower = jnp.where(
        jnp.logical_or(source < half + 16, source >= half + 24), bottom, n_r * 2
    ) - to
    for b in range(5):
        for which, distance in enumerate((upper, lower)):
            coarse = jnp.zeros((half, depth), F32)
            fine = jnp.zeros((half, depth), F32)
            for a in range(5):
                whole = jnp.full((half, depth), weights[a, b])
                rounded = whole.astype(BF16).astype(F32)
                coarse = jnp.where(distance == a - 2, rounded, coarse)
                fine = jnp.where(distance == a - 2, whole - rounded, fine)
            bands[which, b * half : (b + 1) * half] = jnp.concatenate(
                [coarse, fine], axis=1
            ).astype(BF16)

    @pl.when(jnp.logical_not(has_slow))
    def _():
        def clear(j, _):
            e = (HALF - 1 - j) + odd * (n_frame + 1 + 2 * j)
            for slab in (1, 0):
                ext[slab][e] = jnp.zeros((n_r, n_c), F32)
            return 0

        lax.fori_loop(0, HALF, clear, 0)

    def wait_rows(part, slab):
        @pl.when(has_up)
        def _():
            rows_copy(part, slab, 1).wait_recv()

        @pl.when(has_down)
        def _():
            rows_copy(part, slab, 0).wait_recv()

    narrow = lax.broadcasted_iota(jnp.int32, (8, LANES), 1)
    halo_lanes = jnp.where(c == 0, 0, LANES - 2)
    wide = lax.broadcasted_iota(jnp.int32, (16, LANES), 1)
    kept = jnp.logical_and(wide >= halo_lanes, wide < halo_lanes + 2)

    def smooth(slab, f, slot):
        shift = lax.rem(2 * LANES - 2 * f - 2 * c, LANES)
        for i in range(0, n_r + 16, 16):
            moved = pltpu.roll(strip_in[slab, i : i + 16].astype(F32), shift, 1)
            side[i : i + 16] = jnp.where(kept, moved, 0.0).astype(BF16)
        def multiply(part):
            own_rows = slice(part * (half - 16), part * (half - 16) + half + 16)
            for start in range(0, n_c, 2 * LANES):
                columns = slice(start, start + 2 * LANES)
                block = jnp.concatenate(
                    [own[slab][f, own_rows, columns], rows_in[slab, f, :, columns]], axis=0
                )
                shifted[part][:, columns] = jnp.dot(
                    bands[part],
                    jnp.concatenate([block, block], axis=0),
                    preferred_element_type=F32,
                )
            block = jnp.concatenate([side[own_rows], side[n_r : n_r + 16]], axis=0)
            shifted[part][:, n_c : n_c + LANES] = jnp.dot(
                bands[part], jnp.concatenate([block, block], axis=0), preferred_element_type=F32
            )

        def combine(part, at_row):
            def columns(tile):
                parts = []
                for b in range(5):
                    row = at_row + b * half
                    total = shifted[part][row : row + 8, tile * LANES : (tile + 1) * LANES]
                    parts.append(pltpu.roll(total, (2 - b) % LANES, 1) if b != 2 else total)
                return parts

            before = columns(tiles)
            around = before
            here = columns(0)
            to_row = slice(at_row + part * half, at_row + part * half + 8)
            for tile in range(tiles):
                after = columns(tile + 1) if tile + 1 < tiles else around
                value = (
                    here[2]
                    + jnp.where(narrow < 2, before[0], here[0])
                    + jnp.where(narrow < 1, before[1], here[1])
                    + jnp.where(narrow < LANES - 1, here[3], after[3])
                    + jnp.where(narrow < LANES - 2, here[4], after[4])
                )
                columns_of = slice(tile * LANES, (tile + 1) * LANES)
                ext[slab][f + HALF, to_row, columns_of] = value
                slow_out[slab, slot, to_row, columns_of] = value.astype(BF16)
                before, here = here, after

        multiply(0)
        multiply(1)
        for part in (0, 1):
            for at_row in range(0, half, 8):
                combine(part, at_row)

    def slow_copy(slab, j):
        return pltpu.make_async_remote_copy(
            src_ref=slow_out.at[slab, j],
            dst_ref=slow_in.at[slab, j],
            send_sem=slow_send.at[slab, j],
            recv_sem=slow_recv.at[slab, j],
            device_id=at(omega=slow_o),
            device_id_type=MESH,
        )

    def fast_copy(slab, j):
        return pltpu.make_async_remote_copy(
            src_ref=ext[slab].at[fast_frame(j) + HALF],
            dst_ref=ext[slab].at[HALF - 1 - j + odd * (n_frame + 1 + 2 * j)],
            send_sem=fast_send.at[slab, j],
            recv_sem=fast_recv.at[slab, j],
            device_id=at(omega=fast_o),
            device_id_type=MESH,
        )

    def arrive(slab, j):
        slow_copy(slab, j).wait_recv()
        e = (HALF - 1 - j) + odd * (n_frame + 1 + 2 * j)

        def widen(i, _):
            at_row = pl.multiple_of(i * 16, 16)
            ext[slab][e, pl.ds(at_row, 16)] = slow_in[slab, j, pl.ds(at_row, 16)].astype(F32)
            return 0

        lax.fori_loop(0, n_r // 16, widen, 0)

    def wait_fast(slab):
        def wait(j, _):
            fast_copy(slab, j).wait_recv()
            return 0

        lax.fori_loop(0, HALF, wait, 0)

    def load_and_smooth(slab, i):
        for part in range(3):

            @pl.when(i == cuts[part])
            def _():
                load(part, slab).wait()
                wait_rows(part, slab)

        smooth(slab, slow_frame(i), jnp.minimum(i, HALF))

        @pl.when(jnp.logical_and(i < HALF, has_slow))
        def _():
            slow_copy(slab, i).start()

        @pl.when(i >= n_frame - HALF)
        def _():
            fast_copy(slab, n_frame - 1 - i).start()

    def first_slab(i, _):
        load_and_smooth(1, i)
        return 0

    wait_strips(1)
    lax.fori_loop(0, n_frame, first_slab, 0)
    rest = n_frame - HALF

    def filter_frame(slab, f):
        scale = inverse[f]
        for row in range(0, n_r, 8):
            for tile in range(tiles):
                where = (slice(row, row + 8), slice(tile * LANES, (tile + 1) * LANES))
                total = taps[0] * ext[slab][(f,) + where]
                for t in range(1, TAPS):
                    total = total + taps[t] * ext[slab][(f + t,) + where]
                own[slab][(f,) + where] = (ext[slab][(f + HALF,) + where] - total * scale).astype(BF16)

    def filter_slab(slab, start, stop):
        def step(i, _):
            @pl.when(jnp.logical_and(i >= rest, has_slow))
            def _():
                arrive(slab, i - rest)

            filter_frame(slab, slow_frame(jnp.where(i < rest, HALF + i, n_frame - 1 - i)))
            return 0

        lax.fori_loop(start, stop, step, 0)

    def second_slab(i, _):
        load_and_smooth(0, i)
        return 0

    wait_strips(0)
    lax.fori_loop(0, n_frame, second_slab, 0)
    wait_fast(1)
    filter_slab(1, 0, rest)
    wait_fast(0)
    filter_slab(0, 0, rest)
    filter_slab(1, rest, n_frame)

    normalize_patches(own[1], spots, counts, 1, windows, patches, normed, False)
    mirror_copy = pltpu.make_async_remote_copy(
        src_ref=normed,
        dst_ref=mirror,
        send_sem=mirror_send,
        recv_sem=mirror_recv,
        device_id=at(row=n_row - 1 - r, col=1 - c),
        device_id_type=MESH,
    )
    mirror_copy.start()
    filter_slab(0, rest, n_frame)

    mirror_copy.wait()
    for slab in (1, 0):
        each_strip(slab, lambda copy: copy.wait_send())
    for slab in (1, 0):
        for part in range(3):

            @pl.when(has_up)
            def _():
                rows_copy(part, slab, 0).wait_send()

            @pl.when(has_down)
            def _():
                rows_copy(part, slab, 1).wait_send()

        def finish(j, _):
            fast_copy(slab, j).wait_send()

            @pl.when(has_slow)
            def _():
                slow_copy(slab, j).wait_send()

            return 0

        lax.fori_loop(0, HALF, finish, 0)


def layer(sizes, frames, omega_taps, smooth_kernel, spots, counts):
    n_omega, n_row, n_frame, n_r, n_c = sizes
    tiles = n_c // LANES
    n_slot = spots.shape[2]
    hbm = pl.BlockSpec(memory_space=pl.ANY)
    smem = pl.BlockSpec(memory_space=pltpu.SMEM)
    vmem = pl.BlockSpec(memory_space=pltpu.VMEM)
    dma = pltpu.SemaphoreType.DMA
    return pl.pallas_call(
        functools.partial(layer_kernel, sizes),
        out_shape=(
            pltpu.VMEM(frames.shape[1:], BF16),
            pltpu.VMEM(frames.shape[1:], BF16),
            pltpu.VMEM((n_slot, PATCH * PATCH), BF16),
        ),
        in_specs=[hbm, smem, smem, smem, smem],
        out_specs=(vmem, vmem, vmem),
        scratch_shapes=[
            pltpu.VMEM((n_frame + 2 * HALF, n_r, n_c), F32),
            pltpu.VMEM((n_frame + 2 * HALF, n_r, n_c), F32),
            pltpu.VMEM((2, HALF + 1, n_r, n_c), BF16),
            pltpu.VMEM((2, HALF, n_r, n_c), BF16),
            pltpu.VMEM((2, n_frame, 16, n_c), BF16),
            pltpu.VMEM((2, n_frame, n_r, LANES), BF16),
            pltpu.VMEM((2, n_r, LANES), BF16),
            pltpu.VMEM((2, n_r + 16, LANES), BF16),
            pltpu.VMEM((n_r + 16, LANES), BF16),
            pltpu.VMEM((2, 5 * n_r // 2, 2 * (n_r // 2 + 32)), BF16),
            pltpu.VMEM((5 * n_r // 2, n_c + LANES), F32),
            pltpu.VMEM((5 * n_r // 2, n_c + LANES), F32),
            pltpu.VMEM((n_frame, 8, LANES), F32),
            dma((3, 2)),
            dma((2,)),
            dma((2, 3, 2)),
            dma((2, 3, 2)),
            dma((3, 2)),
            dma((3, 2)),
            dma((2, HALF)),
            dma((2, HALF)),
            dma((2, HALF)),
            dma((2, HALF)),
            pltpu.VMEM((8 * 24, LANES), F32),
            pltpu.VMEM((n_slot * PATCH, LANES), F32),
            pltpu.VMEM((n_slot, PATCH * PATCH), BF16),
            dma,
            dma,
        ],
        compiler_params=pltpu.CompilerParams(
            collective_id=0, has_side_effects=True, vmem_limit_bytes=54 * 1024 * 1024
        ),
        name="layer",
    )(frames, omega_taps, smooth_kernel, spots, counts)


def score_kernel(
    held_0, held_1, mirror, spots, counts, out, scores, windows, patches, normed, out_sem
):
    def put(slab):
        return pltpu.make_async_copy((held_0, held_1)[slab], out.at[slab], out_sem.at[slab])

    for slab in (0, 1):
        put(slab).start()
    normalize_patches(held_0, spots, counts, 0, windows, patches, normed, True)
    scores[...] = (
        lax.dot_general(
            normed[...], mirror[...], (((1,), (1,)), ((), ())), preferred_element_type=F32
        )
        / 256.0
    )
    for slab in (0, 1):
        put(slab).wait()


def score(raw, spots, counts, mirror):
    n_slot = mirror.shape[0]
    hbm = pl.BlockSpec(memory_space=pl.ANY)
    smem = pl.BlockSpec(memory_space=pltpu.SMEM)
    vmem = pl.BlockSpec(memory_space=pltpu.VMEM)
    held = [pltpu.with_memory_space_constraint(x, pltpu.VMEM) for x in (*raw, mirror)]
    return pl.pallas_call(
        score_kernel,
        out_shape=(
            jax.ShapeDtypeStruct((2,) + raw[0].shape, BF16),
            jax.ShapeDtypeStruct((n_slot, n_slot), F32),
        ),
        in_specs=[vmem, vmem, vmem, smem, smem],
        out_specs=(hbm, vmem),
        scratch_shapes=[
            pltpu.VMEM((8 * 24, LANES), F32),
            pltpu.VMEM((n_slot * PATCH, LANES), F32),
            pltpu.VMEM((n_slot, PATCH * PATCH), BF16),
            pltpu.SemaphoreType.DMA((2,)),
        ],
        compiler_params=pltpu.CompilerParams(vmem_limit_bytes=16 * 1024 * 1024),
        name="score",
    )(*held, spots, counts)


def solution(mesh):
    n_omega, n_row = (mesh.shape[axis] for axis in ("omega", "row"))

    def shards(frames, omega_taps, smooth_kernel, spots, counts):
        sizes = (n_omega, n_row) + frames.shape[1:]
        spots = jnp.transpose(spots, (1, 0, 2))
        counts = jnp.transpose(counts, (1, 0))
        *raw, mirror = layer(sizes, frames, omega_taps, smooth_kernel, spots, counts)
        smoothed, scores = score(raw, spots, counts, mirror)
        return (smoothed, scores)

    return jax.shard_map(
        shards,
        mesh=mesh,
        in_specs=(
            P(None, "omega", "row", "col"),
            P(),
            P(),
            P(None, None, ("omega", "row", "col")),
            P(None, ("omega", "row", "col")),
        ),
        out_specs=(P(None, "omega", "row", "col"), P(("omega", "row", "col"), None)),
        check_vma=False,
    )
```

```python
import functools

import jax
import jax.numpy as jnp
from jax import lax
from jax.experimental import pallas as pl
from jax.experimental.pallas import tpu as pltpu
from jax.sharding import PartitionSpec as P

TAPS = 15
PATCH = 16
HALF = 7
LANES = 128
MESH = pl.DeviceIdType.MESH
F32 = jnp.float32
BF16 = jnp.bfloat16


def normalize_patches(held, spots, counts, slab, windows, patches, normed, by_amount):
    n_frame, n_r, n_c = held.shape
    n_slot = normed.shape[0]
    lane = lax.broadcasted_iota(jnp.int32, (24, LANES), 1)
    group = lax.broadcasted_iota(jnp.int32, (n_slot, LANES), 1)
    slot = lax.broadcasted_iota(jnp.int32, (n_slot, 1), 0)

    def one(i, _):
        f = spots[0, slab, i] & (n_frame - 1)
        row = spots[1, slab, i] & (n_r - 1)
        col = spots[2, slab, i] & (n_c - 1)
        row_0 = jnp.minimum(row >> 3, n_r // 8 - 3) * 8
        col_0 = jnp.minimum(col >> 7, n_c // LANES - 2) * LANES
        shift = col - col_0
        window = held[f, pl.ds(row_0, 24), pl.ds(col_0, 2 * LANES)].astype(F32)
        left, right = window[:, :LANES], window[:, LANES:]
        if by_amount:
            turn = (2 * LANES - shift) & (LANES - 1)
            left = jnp.where(
                lane < LANES - shift, pltpu.roll(left, turn, 1), pltpu.roll(right, turn, 1)
            )
        else:
            left = jnp.where(shift >= LANES, right, left)
            for bit in (64, 32, 16, 8, 4, 2, 1):
                on = (shift & bit) != 0
                moved_left = pltpu.roll(left, LANES - bit, 1)
                moved_right = pltpu.roll(right, LANES - bit, 1)
                left = jnp.where(on, jnp.where(lane < LANES - bit, moved_left, moved_right), left)
                right = jnp.where(on, moved_right, right)
        at_window = (i & 15) * 24
        windows[pl.ds(at_window, 24)] = left
        patches[pl.ds(i * PATCH, PATCH)] = windows[pl.ds(at_window + (row - row_0), PATCH)]
        return 0

    lax.fori_loop(0, n_slot, one, 0, unroll=16)
    halves = []
    for half in range(2):
        total = jnp.zeros((n_slot, LANES), F32)
        for u in range(8):
            line = patches[pl.ds(half * 8 + u, n_slot, stride=PATCH)]
            line = pltpu.roll(line, PATCH * u, 1) if u else line
            total = jnp.where(
                jnp.logical_and(group >= PATCH * u, group < PATCH * (u + 1)), line, total
            )
        halves.append(total)
    values = jnp.concatenate(halves, axis=1)
    mean = jnp.mean(values, axis=1, keepdims=True)
    centered = values - mean
    spread = jnp.mean(centered * centered, axis=1, keepdims=True)
    result = centered / jnp.sqrt(spread + 1e-05)
    normed[...] = jnp.where(slot < counts[0, slab], result, 0.0).astype(BF16)


def layer_kernel(
    sizes,
    frames,
    taps,
    weights,
    spots,
    counts,
    own_0,
    own_1,
    mirror,
    ext_0,
    ext_1,
    slow_out,
    slow_in,
    rows_in,
    edge,
    strip,
    strip_in,
    side,
    bands,
    shifted_0,
    shifted_1,
    inverse,
    load_sem,
    edge_sem,
    rows_send,
    rows_recv,
    strip_send,
    strip_recv,
    slow_send,
    slow_recv,
    fast_send,
    fast_recv,
    windows,
    patches,
    normed,
    mirror_send,
    mirror_recv,
):
    n_omega, n_row, n_frame, n_r, n_c = sizes
    shifted = (shifted_0, shifted_1)
    ext = (ext_0, ext_1)
    own = (own_0, own_1)
    tiles = n_c // LANES
    o = lax.axis_index("omega")
    r = lax.axis_index("row")
    c = lax.axis_index("col")
    odd = lax.rem(o, 2)
    slow_o = o - 1 + 2 * odd
    fast_o = o + 1 - 2 * odd
    has_slow = jnp.logical_and(slow_o >= 0, slow_o < n_omega)
    has_up = r > 0
    has_down = r < n_row - 1

    def at(omega=o, row=r, col=c):
        return {"omega": omega, "row": row, "col": col}

    def slow_frame(j):
        return j + odd * (n_frame - 1 - 2 * j)

    def fast_frame(j):
        return slow_frame(n_frame - 1 - j)

    cuts = (0, 2, HALF, n_frame)
    order = [(slab, part) for slab in (1, 0) for part in range(3)]

    def stretch(part):
        start, stop = cuts[part], cuts[part + 1]
        return start + odd * (n_frame - stop - start), stop - start

    def edge_copy(slab):
        return pltpu.make_async_copy(
            frames.at[slab, :, :, pl.ds(pl.multiple_of((1 - c) * (n_c - LANES), LANES), LANES)],
            edge.at[slab],
            edge_sem.at[slab],
        )

    for slab in (1, 0):
        edge_copy(slab).start()

    def load(part, slab):
        first, count = stretch(part)
        return pltpu.make_async_copy(
            frames.at[slab, pl.ds(first, count)],
            own[slab].at[pl.ds(first, count)],
            load_sem.at[part, slab],
        )

    barrier = pltpu.get_barrier_semaphore()

    def greet(device):
        pl.semaphore_signal(barrier, inc=1, device_id=device, device_id_type=MESH)

    greet(at(omega=fast_o))
    greet(at(col=1 - c))
    greet(at(row=n_row - 1 - r, col=1 - c))

    @pl.when(has_slow)
    def _():
        greet(at(omega=slow_o))

    @pl.when(has_up)
    def _():
        greet(at(row=r - 1))
        greet(at(row=r - 1, col=1 - c))

    @pl.when(has_down)
    def _():
        greet(at(row=r + 1))
        greet(at(row=r + 1, col=1 - c))

    lane = lax.broadcasted_iota(jnp.int32, (n_r, LANES), 1)

    def pack(slab):
        edge_copy(slab).wait()

        def gather(f, packed):
            moved = pltpu.roll(edge[slab, f].astype(F32), 2 * f + 2 * (1 - c), 1)
            return jnp.where(jnp.logical_and(lane >= 2 * f, lane < 2 * f + 2), moved, packed)

        packed = lax.fori_loop(0, n_frame, gather, jnp.zeros((n_r, LANES), F32), unroll=4)
        strip[slab] = packed.astype(BF16)

    pack(1)
    pl.semaphore_wait(
        barrier,
        3
        + has_slow.astype(jnp.int32)
        + 2 * has_up.astype(jnp.int32)
        + 2 * has_down.astype(jnp.int32),
    )

    def strip_copy(which, slab):
        source, target, row = (
            (pl.ds(0, n_r), pl.ds(0, n_r), r),
            (pl.ds(0, 8), pl.ds(n_r + 8, 8), r - 1),
            (pl.ds(n_r - 8, 8), pl.ds(n_r, 8), r + 1),
        )[which]
        return pltpu.make_async_remote_copy(
            src_ref=strip.at[slab, source],
            dst_ref=strip_in.at[slab, target],
            send_sem=strip_send.at[which, slab],
            recv_sem=strip_recv.at[which, slab],
            device_id=at(row=row, col=1 - c),
            device_id_type=MESH,
        )

    def each_strip(slab, act):
        act(strip_copy(0, slab))

        @pl.when(has_up)
        def _():
            act(strip_copy(1, slab))

        @pl.when(has_down)
        def _():
            act(strip_copy(2, slab))

    def wait_strips(slab):
        strip_copy(0, slab).wait_recv()

        @pl.when(has_down)
        def _():
            strip_copy(1, slab).wait_recv()

        @pl.when(has_up)
        def _():
            strip_copy(2, slab).wait_recv()

    each_strip(1, lambda copy: copy.start())

    def rows_copy(part, slab, down):
        first, count = stretch(part)
        return pltpu.make_async_remote_copy(
            src_ref=frames.at[slab, pl.ds(first, count), pl.ds((n_r - 8) * down, 8)],
            dst_ref=rows_in.at[slab, pl.ds(first, count), pl.ds(8 * (1 - down), 8)],
            send_sem=rows_send.at[down, part, slab],
            recv_sem=rows_recv.at[1 - down, part, slab],
            device_id=at(row=r + 2 * down - 1),
            device_id_type=MESH,
        )

    for slab, part in order:

        @pl.when(has_up)
        def _():
            rows_copy(part, slab, 0).start()

        @pl.when(has_down)
        def _():
            rows_copy(part, slab, 1).start()

    for slab, part in order:
        load(part, slab).start()
    pack(0)
    each_strip(0, lambda copy: copy.start())

    @pl.when(jnp.logical_not(has_up))
    def _():
        rows_in[:, :, pl.ds(0, 8)] = jnp.zeros((2, n_frame, 8, n_c), BF16)
        strip_in[:, pl.ds(n_r, 8)] = jnp.zeros((2, 8, LANES), BF16)

    @pl.when(jnp.logical_not(has_down))
    def _():
        rows_in[:, :, pl.ds(8, 8)] = jnp.zeros((2, n_frame, 8, n_c), BF16)
        strip_in[:, pl.ds(n_r + 8, 8)] = jnp.zeros((2, 8, LANES), BF16)

    for f in range(n_frame):
        norm = jnp.zeros((8, LANES), F32)
        for t in range(TAPS):
            source = o * n_frame + (f + t - HALF)
            valid = jnp.logical_and(source >= 0, source < n_omega * n_frame)
            norm = norm + jnp.where(valid, taps[t], 0.0)
        inverse[f] = 1.0 / norm

    half = n_r // 2
    depth = half + 32
    to = lax.broadcasted_iota(jnp.int32, (half, depth), 0)
    source = lax.broadcasted_iota(jnp.int32, (half, depth), 1)
    top = jnp.where(source < half + 16, source, source - (half + 24))
    bottom = jnp.where(source < half + 16, source - 16, source - 24)
    upper = jnp.where(source < half + 24, top, n_r * 2) - to
    lower = jnp.where(
        jnp.logical_or(source < half + 16, source >= half + 24), bottom, n_r * 2
    ) - to
    for b in range(5):
        for which, distance in enumerate((upper, lower)):
            coarse = jnp.zeros((half, depth), F32)
            fine = jnp.zeros((half, depth), F32)
            for a in range(5):
                whole = jnp.full((half, depth), weights[a, b])
                rounded = whole.astype(BF16).astype(F32)
                coarse = jnp.where(distance == a - 2, rounded, coarse)
                fine = jnp.where(distance == a - 2, whole - rounded, fine)
            bands[which, b * half : (b + 1) * half] = jnp.concatenate(
                [coarse, fine], axis=1
            ).astype(BF16)

    @pl.when(jnp.logical_not(has_slow))
    def _():
        def clear(j, _):
            e = (HALF - 1 - j) + odd * (n_frame + 1 + 2 * j)
            for slab in (1, 0):
                ext[slab][e] = jnp.zeros((n_r, n_c), F32)
            return 0

        lax.fori_loop(0, HALF, clear, 0)

    def wait_rows(part, slab):
        @pl.when(has_up)
        def _():
            rows_copy(part, slab, 1).wait_recv()

        @pl.when(has_down)
        def _():
            rows_copy(part, slab, 0).wait_recv()

    narrow = lax.broadcasted_iota(jnp.int32, (8, LANES), 1)
    halo_lanes = jnp.where(c == 0, 0, LANES - 2)
    wide = lax.broadcasted_iota(jnp.int32, (16, LANES), 1)
    kept = jnp.logical_and(wide >= halo_lanes, wide < halo_lanes + 2)

    def smooth(slab, f, slot):
        shift = lax.rem(2 * LANES - 2 * f - 2 * c, LANES)
        for i in range(0, n_r + 16, 16):
            moved = pltpu.roll(strip_in[slab, i : i + 16].astype(F32), shift, 1)
            side[i : i + 16] = jnp.where(kept, moved, 0.0).astype(BF16)
        def multiply(part):
            own_rows = slice(part * (half - 16), part * (half - 16) + half + 16)
            for start in range(0, n_c, 2 * LANES):
                columns = slice(start, start + 2 * LANES)
                block = jnp.concatenate(
                    [own[slab][f, own_rows, columns], rows_in[slab, f, :, columns]], axis=0
                )
                shifted[part][:, columns] = jnp.dot(
                    bands[part],
                    jnp.concatenate([block, block], axis=0),
                    preferred_element_type=F32,
                )
            block = jnp.concatenate([side[own_rows], side[n_r : n_r + 16]], axis=0)
            shifted[part][:, n_c : n_c + LANES] = jnp.dot(
                bands[part], jnp.concatenate([block, block], axis=0), preferred_element_type=F32
            )

        def combine(part, at_row):
            def columns(tile):
                parts = []
                for b in range(5):
                    row = at_row + b * half
                    total = shifted[part][row : row + 8, tile * LANES : (tile + 1) * LANES]
                    parts.append(pltpu.roll(total, (2 - b) % LANES, 1) if b != 2 else total)
                return parts

            before = columns(tiles)
            around = before
            here = columns(0)
            to_row = slice(at_row + part * half, at_row + part * half + 8)
            for tile in range(tiles):
                after = columns(tile + 1) if tile + 1 < tiles else around
                value = (
                    here[2]
                    + jnp.where(narrow < 2, before[0], here[0])
                    + jnp.where(narrow < 1, before[1], here[1])
                    + jnp.where(narrow < LANES - 1, here[3], after[3])
                    + jnp.where(narrow < LANES - 2, here[4], after[4])
                )
                columns_of = slice(tile * LANES, (tile + 1) * LANES)
                ext[slab][f + HALF, to_row, columns_of] = value
                slow_out[slab, slot, to_row, columns_of] = value.astype(BF16)
                before, here = here, after

        multiply(0)
        multiply(1)
        for part in (0, 1):
            for at_row in range(0, half, 8):
                combine(part, at_row)

    def slow_copy(slab, j):
        return pltpu.make_async_remote_copy(
            src_ref=slow_out.at[slab, j],
            dst_ref=slow_in.at[slab, j],
            send_sem=slow_send.at[slab, j],
            recv_sem=slow_recv.at[slab, j],
            device_id=at(omega=slow_o),
            device_id_type=MESH,
        )

    def fast_copy(slab, j):
        return pltpu.make_async_remote_copy(
            src_ref=ext[slab].at[fast_frame(j) + HALF],
            dst_ref=ext[slab].at[HALF - 1 - j + odd * (n_frame + 1 + 2 * j)],
            send_sem=fast_send.at[slab, j],
            recv_sem=fast_recv.at[slab, j],
            device_id=at(omega=fast_o),
            device_id_type=MESH,
        )

    def arrive(slab, j):
        slow_copy(slab, j).wait_recv()
        e = (HALF - 1 - j) + odd * (n_frame + 1 + 2 * j)

        def widen(i, _):
            at_row = pl.multiple_of(i * 16, 16)
            ext[slab][e, pl.ds(at_row, 16)] = slow_in[slab, j, pl.ds(at_row, 16)].astype(F32)
            return 0

        lax.fori_loop(0, n_r // 16, widen, 0)

    def wait_fast(slab):
        def wait(j, _):
            fast_copy(slab, j).wait_recv()
            return 0

        lax.fori_loop(0, HALF, wait, 0)

    def load_and_smooth(slab, i):
        for part in range(3):

            @pl.when(i == cuts[part])
            def _():
                load(part, slab).wait()
                wait_rows(part, slab)

        smooth(slab, slow_frame(i), jnp.minimum(i, HALF))

        @pl.when(jnp.logical_and(i < HALF, has_slow))
        def _():
            slow_copy(slab, i).start()

        @pl.when(i >= n_frame - HALF)
        def _():
            fast_copy(slab, n_frame - 1 - i).start()

    def first_slab(i, _):
        load_and_smooth(1, i)
        return 0

    wait_strips(1)
    lax.fori_loop(0, n_frame, first_slab, 0)
    rest = n_frame - HALF

    def filter_frame(slab, f):
        scale = inverse[f]
        for row in range(0, n_r, 8):
            for tile in range(tiles):
                where = (slice(row, row + 8), slice(tile * LANES, (tile + 1) * LANES))
                total = taps[0] * ext[slab][(f,) + where]
                for t in range(1, TAPS):
                    total = total + taps[t] * ext[slab][(f + t,) + where]
                own[slab][(f,) + where] = (ext[slab][(f + HALF,) + where] - total * scale).astype(BF16)

    def filter_slab(slab, start, stop):
        def step(i, _):
            @pl.when(jnp.logical_and(i >= rest, has_slow))
            def _():
                arrive(slab, i - rest)

            filter_frame(slab, slow_frame(jnp.where(i < rest, HALF + i, n_frame - 1 - i)))
            return 0

        lax.fori_loop(start, stop, step, 0)

    def second_slab(i, _):
        load_and_smooth(0, i)
        return 0

    wait_strips(0)
    lax.fori_loop(0, n_frame, second_slab, 0)
    wait_fast(1)
    filter_slab(1, 0, rest)
    wait_fast(0)
    filter_slab(0, 0, rest)
    filter_slab(1, rest, n_frame)

    normalize_patches(own[1], spots, counts, 1, windows, patches, normed, False)
    mirror_copy = pltpu.make_async_remote_copy(
        src_ref=normed,
        dst_ref=mirror,
        send_sem=mirror_send,
        recv_sem=mirror_recv,
        device_id=at(row=n_row - 1 - r, col=1 - c),
        device_id_type=MESH,
    )
    mirror_copy.start()
    for slab in (1, 0):
        each_strip(slab, lambda copy: copy.wait_send())
    for slab in (1, 0):
        for part in range(3):

            @pl.when(has_up)
            def _():
                rows_copy(part, slab, 0).wait_send()

            @pl.when(has_down)
            def _():
                rows_copy(part, slab, 1).wait_send()

        def finish(j, _):
            fast_copy(slab, j).wait_send()
            return 0

        lax.fori_loop(0, HALF, finish, 0)

    filter_slab(0, rest, n_frame)

    mirror_copy.wait()
    @pl.when(has_slow)
    def _():
        def sent(j, _):
            for slab in (1, 0):
                slow_copy(slab, j).wait_send()
            return 0

        lax.fori_loop(0, HALF, sent, 0)


def layer(sizes, frames, omega_taps, smooth_kernel, spots, counts):
    n_omega, n_row, n_frame, n_r, n_c = sizes
    tiles = n_c // LANES
    n_slot = spots.shape[2]
    hbm = pl.BlockSpec(memory_space=pl.ANY)
    smem = pl.BlockSpec(memory_space=pltpu.SMEM)
    vmem = pl.BlockSpec(memory_space=pltpu.VMEM)
    dma = pltpu.SemaphoreType.DMA
    return pl.pallas_call(
        functools.partial(layer_kernel, sizes),
        out_shape=(
            pltpu.VMEM(frames.shape[1:], BF16),
            pltpu.VMEM(frames.shape[1:], BF16),
            pltpu.VMEM((n_slot, PATCH * PATCH), BF16),
        ),
        in_specs=[hbm, smem, smem, smem, smem],
        out_specs=(vmem, vmem, vmem),
        scratch_shapes=[
            pltpu.VMEM((n_frame + 2 * HALF, n_r, n_c), F32),
            pltpu.VMEM((n_frame + 2 * HALF, n_r, n_c), F32),
            pltpu.VMEM((2, HALF + 1, n_r, n_c), BF16),
            pltpu.VMEM((2, HALF, n_r, n_c), BF16),
            pltpu.VMEM((2, n_frame, 16, n_c), BF16),
            pltpu.VMEM((2, n_frame, n_r, LANES), BF16),
            pltpu.VMEM((2, n_r, LANES), BF16),
            pltpu.VMEM((2, n_r + 16, LANES), BF16),
            pltpu.VMEM((n_r + 16, LANES), BF16),
            pltpu.VMEM((2, 5 * n_r // 2, 2 * (n_r // 2 + 32)), BF16),
            pltpu.VMEM((5 * n_r // 2, n_c + LANES), F32),
            pltpu.VMEM((5 * n_r // 2, n_c + LANES), F32),
            pltpu.VMEM((n_frame, 8, LANES), F32),
            dma((3, 2)),
            dma((2,)),
            dma((2, 3, 2)),
            dma((2, 3, 2)),
            dma((3, 2)),
            dma((3, 2)),
            dma((2, HALF)),
            dma((2, HALF)),
            dma((2, HALF)),
            dma((2, HALF)),
            pltpu.VMEM((16 * 24, LANES), F32),
            pltpu.VMEM((n_slot * PATCH, LANES), F32),
            pltpu.VMEM((n_slot, PATCH * PATCH), BF16),
            dma,
            dma,
        ],
        compiler_params=pltpu.CompilerParams(
            collective_id=0, has_side_effects=True, vmem_limit_bytes=54 * 1024 * 1024
        ),
        name="layer",
    )(frames, omega_taps, smooth_kernel, spots, counts)


def score_kernel(
    held_0, held_1, mirror, spots, counts, out, scores, windows, patches, normed, out_sem
):
    def put(slab):
        return pltpu.make_async_copy((held_0, held_1)[slab], out.at[slab], out_sem.at[slab])

    for slab in (0, 1):
        put(slab).start()
    normalize_patches(held_0, spots, counts, 0, windows, patches, normed, True)
    scores[...] = (
        lax.dot_general(
            normed[...], mirror[...], (((1,), (1,)), ((), ())), preferred_element_type=F32
        )
        / 256.0
    )
    for slab in (0, 1):
        put(slab).wait()


def score(raw, spots, counts, mirror):
    n_slot = mirror.shape[0]
    hbm = pl.BlockSpec(memory_space=pl.ANY)
    smem = pl.BlockSpec(memory_space=pltpu.SMEM)
    vmem = pl.BlockSpec(memory_space=pltpu.VMEM)
    held = [pltpu.with_memory_space_constraint(x, pltpu.VMEM) for x in (*raw, mirror)]
    return pl.pallas_call(
        score_kernel,
        out_shape=(
            jax.ShapeDtypeStruct((2,) + raw[0].shape, BF16),
            jax.ShapeDtypeStruct((n_slot, n_slot), F32),
        ),
        in_specs=[vmem, vmem, vmem, smem, smem],
        out_specs=(hbm, vmem),
        scratch_shapes=[
            pltpu.VMEM((16 * 24, LANES), F32),
            pltpu.VMEM((n_slot * PATCH, LANES), F32),
            pltpu.VMEM((n_slot, PATCH * PATCH), BF16),
            pltpu.SemaphoreType.DMA((2,)),
        ],
        compiler_params=pltpu.CompilerParams(vmem_limit_bytes=16 * 1024 * 1024),
        name="score",
    )(*held, spots, counts)


def solution(mesh):
    n_omega, n_row = (mesh.shape[axis] for axis in ("omega", "row"))

    def shards(frames, omega_taps, smooth_kernel, spots, counts):
        sizes = (n_omega, n_row) + frames.shape[1:]
        spots = jnp.transpose(spots, (1, 0, 2))
        counts = jnp.transpose(counts, (1, 0))
        *raw, mirror = layer(sizes, frames, omega_taps, smooth_kernel, spots, counts)
        smoothed, scores = score(raw, spots, counts, mirror)
        return (smoothed, scores)

    return jax.shard_map(
        shards,
        mesh=mesh,
        in_specs=(
            P(None, "omega", "row", "col"),
            P(),
            P(),
            P(None, None, ("omega", "row", "col")),
            P(None, ("omega", "row", "col")),
        ),
        out_specs=(P(None, "omega", "row", "col"), P(("omega", "row", "col"), None)),
        check_vma=False,
    )
```
